32 devices in a mesh: prow: 8 (over y, x, core), pcol: 4 (over z).
Axes of the slice: x: 2, y: 2, z: 4, core: 2. Of those that a mesh axis runs over, the one named last changes fastest.
Arguments:
- u_window: float32 [6, 8, 512, 4, 4, 512], P(None, 'prow', None, None, 'pcol'), may hold values from -0.625 to 0.625
Outputs:
- lauum_columns: float32 [1024, 6, 8, 512], P('pcol', None, 'prow')
The draws below stay inside these ranges and needn't reach their ends.
All inputs are finite; a program needn't handle non-finite values.
Results may differ from the reference program's by a relative error of at most 0.000061.
Values sent between devices are 32-bit elements; how exact they have to be, the bound alone decides.
A program may use at most 192 MiB of HBM per device.

```python
import jax
import jax.numpy as jnp
from jax import lax

NB = 512
RB = 6
CB = 4
N_PROW = 8
N_PCOL = 4


def level_of(key, shape, split, least, top_value):
    gain, own = 1.0, jax.random.fold_in(key, 6)
    for axis_at, blocks in split:
        heights = jnp.exp(jax.random.uniform(jax.random.fold_in(own, axis_at), (blocks,), jnp.float32, least / len(split), top_value / len(split)))
        gain = gain * jnp.repeat(heights, shape[axis_at] // blocks).reshape([-1 if axis == axis_at else 1 for axis in range(len(shape))])
    return gain


def normal_values(key, dims, width, limit, cuts=(), held_as=jnp.bfloat16):
    values = width * jax.random.normal(key, dims, jnp.float32)
    if cuts:
        values = values * level_of(key, dims, cuts, -0.22, 0.18)
    return jnp.clip(values, -limit, limit).astype(held_as)


def setup_inputs(seed: int = 0) -> dict:
    splits = jax.random.split(jax.random.key(seed), 2)
    return {
        "u_window": normal_values(splits[0], (RB, N_PROW, NB, CB, N_PCOL, NB), ((CB * N_PCOL * NB) ** -0.25), 0.625, ((1, 8), (4, 4)), jnp.float32),
    }


def contract(left, right):
    return lax.dot_general(left, right, (((1,), (1,)), ((), ())), precision=lax.Precision.HIGHEST, preferred_element_type=jnp.float32)


def reference(u_window):
    height = RB * N_PROW
    width_cols = CB * N_PCOL * NB
    matrix = u_window.reshape(height * NB, width_cols)
    anchor = (height - 2) * NB
    panel_rows = matrix[anchor:]
    row_ids = jnp.arange(2 * NB, dtype=jnp.int32)
    col_ids = jnp.arange(width_cols, dtype=jnp.int32)
    masked = jnp.where(row_ids[:, None] <= col_ids[None, :], panel_rows, jnp.zeros_like(panel_rows))
    product = jnp.concatenate([contract(masked, matrix[:anchor]), contract(masked, masked)], 1)
    return product.reshape(2 * NB, RB, N_PROW, NB)
```

```python
import jax
import jax.numpy as jnp
from jax import lax
from jax.sharding import PartitionSpec as P

CHUNKS = 4


def contract(left, right):
    return lax.dot_general(
        left,
        right,
        (((1,), (1,)), ((), ())),
        precision=lax.Precision.HIGH,
        preferred_element_type=jnp.float32,
    )


def walks(prow_size):
    bits = (prow_size // 2).bit_length() - 1
    gray = [step ^ (step >> 1) for step in range(prow_size // 2)]
    mirrored = [sum(((g >> b) & 1) << (bits - 1 - b) for b in range(bits)) for g in gray]
    even = [(prow_size - 2) ^ (g << 1) for g in gray]
    odd = [(prow_size - 1) ^ (g << 1) for g in mirrored]
    return even, odd


def on_device(u_window):
    row_blocks = u_window.shape[0]
    block_size = u_window.shape[2]
    col_blocks = u_window.shape[3]
    prow_size = lax.axis_size("prow")
    pcol_size = lax.axis_size("pcol")
    my_row = lax.axis_index("prow")
    my_col = lax.axis_index("pcol")
    width = col_blocks * block_size
    anchor = (row_blocks * prow_size - 2) * block_size
    row_ids = ((row_blocks - 1) * prow_size + my_row) * block_size + jnp.arange(
        block_size, dtype=jnp.int32
    )
    col_index = jnp.arange(width, dtype=jnp.int32)
    window_col = (
        col_index // block_size * pcol_size + my_col
    ) * block_size + col_index % block_size
    last_row = u_window[row_blocks - 1].reshape(block_size, width)
    masked = jnp.where(
        row_ids[:, None] <= anchor + window_col[None, :], last_row, jnp.zeros_like(last_row)
    )
    all_index = jnp.arange(row_blocks * block_size, dtype=jnp.int32)
    all_ids = (
        all_index // block_size * prow_size + my_row
    ) * block_size + all_index % block_size
    blocks = u_window.reshape(row_blocks * block_size, width)
    window = lax.optimization_barrier(
        jnp.where(all_ids[:, None] <= anchor + window_col[None, :], blocks, jnp.zeros_like(blocks))
    )

    owners = pcol_size // 2
    part = block_size // owners // CHUNKS
    by_chunk = masked.reshape(owners, CHUNKS, part, width)
    chunks = [by_chunk[:, chunk].reshape(owners * part, width) for chunk in range(CHUNKS)]
    even, odd = walks(prow_size)
    place = [max(even.index(row) if row in even else 0, odd.index(row) if row in odd else 0) for row in range(prow_size)]
    my_place = jnp.asarray(place, jnp.int32)[my_row]
    is_even = my_row % 2 == 0
    swap = [(row, row ^ 1) for row in range(prow_size)]
    links = list(zip(even[:-1], even[1:])) + list(zip(odd[:-1], odd[1:]))
    hops = len(even) - 1
    got, partials, results = [], [], []
    for wave in range(CHUNKS + hops - 1):
        fresh = chunks[min(wave, CHUNKS - 1)]
        send = jnp.where(my_place == 0, fresh, got[-1]) if got else fresh
        if len(partials) > 1:
            send, partials[-2] = lax.optimization_barrier((send, partials[-2]))
        elif partials:
            send, panels = lax.optimization_barrier((send, panels))
        got.append(lax.ppermute(send, "prow", links))
        chunk = wave - hops + 1
        if chunk < 0:
            continue
        own = chunks[chunk]
        for hop in range(hops):
            own = jnp.where(my_place == hop + 1, got[chunk + hop], own)
        other = lax.ppermute(own, "prow", swap)
        panels = jnp.concatenate(
            [jnp.where(is_even, own, other), jnp.where(is_even, other, own)], 0
        )
        if partials:
            panels, partials[-1] = lax.optimization_barrier((panels, partials[-1]))
        partials.append(contract(panels, window))
    for partial in partials:
        results.append(lax.psum_scatter(partial, "pcol", scatter_dimension=0, tiled=True))
    summed = jnp.concatenate(results, 0)
    return summed.reshape(summed.shape[0], row_blocks, 1, block_size)


def solution(mesh):
    placed = (P(None, "prow", None, None, "pcol", None),)
    return jax.shard_map(
        on_device,
        mesh=mesh,
        in_specs=placed,
        out_specs=P("pcol", None, "prow", None),
        check_vma=False,
    )
```
